128 devices in a mesh: shard: 64 (over z, y, x), tensor: 2 (over core).
Axes of the slice: x: 4, y: 4, z: 4, core: 2. Of those that a mesh axis runs over, the one named last changes fastest.
Arguments:
- weights: float32 [128, 512, 512], P(None, 'shard', 'tensor'), may hold values from -0.25 to 0.25
- gradient: float32 [128, 512, 512], P(None, 'shard', 'tensor'), may hold values from -40 to 40
- first_moment: float32 [128, 512, 512], P(None, 'shard', 'tensor'), may hold values from -6 to 6
- second_moment: float32 [128, 512, 512], P(None, 'shard', 'tensor'), may hold values from 0.25 to 4
- left_stat: float32 [128, 512, 512], P(None, 'shard', 'tensor'), may hold values from -4 to 16, as said below
- right_stat: float32 [128, 512, 512], P(None, 'shard', 'tensor'), may hold values from -4 to 16, as said below
- left_basis: float32 [128, 512, 512], P(None, 'shard', 'tensor'), may hold values from -0.7 to 1.7
- right_basis: float32 [128, 512, 512], P(None, 'shard', 'tensor'), may hold values from -0.7 to 1.7
Outputs:
- new_weights: float32 [128, 512, 512], P(None, 'shard', 'tensor')
- new_first: float32 [128, 512, 512], P(None, 'shard', 'tensor')
- new_second: float32 [128, 512, 512], P(None, 'shard', 'tensor')
- new_left_stat: float32 [128, 512, 512], P(None, 'shard', 'tensor')
- new_right_stat: float32 [128, 512, 512], P(None, 'shard', 'tensor')
- new_left_basis: float32 [128, 512, 512], P(None, 'shard', 'tensor')
- new_right_basis: float32 [128, 512, 512], P(None, 'shard', 'tensor')
The draws below stay inside these ranges and needn't reach their ends.
Inputs may be any that keep to these rules, and one draw needn't show every extreme that they name: `left_stat`: symmetric. `right_stat`: symmetric.
All inputs are finite; a program needn't handle non-finite values.
Results may differ from the reference program's by a relative error of at most 0.0003.
Values sent between devices are 32-bit elements; how exact they have to be, the bound alone decides.
A program may use at most 128 MiB of HBM per device.

```python
import math
import jax
import jax.numpy as jnp
from jax import lax

D = 512
NS_STEPS = 5
MATS = 128


def index_ramp(low, high):
    position = jnp.arange(D, dtype=jnp.float32) / float(D - 1)
    return jnp.exp(math.log(low) + (math.log(high) - math.log(low)) * position)


def draw_gradient(key, part):
    keys = jax.random.split(jax.random.fold_in(key, 11), 3)
    rowscale = jnp.exp(jax.random.uniform(keys[0], (MATS, D, 1), minval=math.log(0.3), maxval=math.log(3.0)))
    colrand = jnp.exp(jax.random.uniform(keys[1], (MATS, 1, D), minval=math.log(0.5), maxval=math.log(1.8)))
    colscale = colrand * index_ramp(0.6, 1.8)[None, None, :]
    base = jnp.clip(jax.random.normal(keys[2], (MATS, D, D)), -4.0, 4.0)
    return (base * rowscale * colscale).astype(jnp.float32)


def symmetric_stat(key):
    keys = jax.random.split(key, 2)
    scales = jnp.exp(jax.random.uniform(keys[0], (MATS, D), minval=0.0, maxval=math.log(1.8))) * index_ramp(1.0, math.sqrt(3.0))[None, :]
    noise = jnp.clip(jax.random.normal(keys[1], (MATS, D, D)), -4.0, 4.0)
    offdiag = 0.03 * (noise + jnp.swapaxes(noise, 1, 2)) / math.sqrt(2.0)
    ident = jnp.eye(D, dtype=jnp.float32)
    matrix = ident + offdiag * (1.0 - ident)
    return (matrix * scales[:, :, None] * scales[:, None, :]).astype(jnp.float32)


def draw_left_stat(key, part):
    return symmetric_stat(jax.random.fold_in(key, 21))


def draw_right_stat(key, part):
    return symmetric_stat(jax.random.fold_in(key, 22))


def near_basis(key):
    ident = jnp.eye(D, dtype=jnp.float32)
    spread = 1.2 / math.sqrt(D)
    noise = jnp.clip(jax.random.normal(key, (MATS, D, D)), -4.0, 4.0)
    return (ident + spread * noise).astype(jnp.float32)


def draw_left_basis(key, part):
    return near_basis(jax.random.fold_in(key, 31))


def draw_right_basis(key, part):
    return near_basis(jax.random.fold_in(key, 32))


def shard_levels(key, extent, cuts, least, top_value):
    def one(dim, blocks):
        heights = jax.random.uniform(jax.random.fold_in(jax.random.fold_in(key, 6), dim), (blocks,), jnp.float32, least / len(cuts), top_value / len(cuts))
        return jnp.repeat(jnp.exp(heights), extent[dim] // blocks).reshape((-1,) + (1,) * (len(extent) - dim - 1))

    level = one(*cuts[0])
    for cut in cuts[1:]:
        level = level * one(*cut)
    return level


def gaussian(key, dims, scale, most, shards=(), held_as=jnp.bfloat16):
    values = scale * jax.random.normal(key, dims, jnp.float32)
    if shards:
        values = values * shard_levels(key, dims, shards, -0.22, 0.18)
    return jnp.clip(values, -most, most).astype(held_as)


def setup_inputs(seed: int = 0) -> dict:
    seeds = jax.random.split(jax.random.key(seed), 9)
    weights = gaussian(seeds[0], (MATS, D, D), D ** -0.5, 0.25, ((1, 64), (2, 2)), jnp.float32)
    gradient = draw_gradient(jax.random.fold_in(seeds[8], 71), 0)
    first_moment = gaussian(seeds[2], (MATS, D, D), 1.0, 6.0, ((1, 64), (2, 2)), jnp.float32)
    second_moment = jnp.clip(jnp.exp(math.log(4.0) - 2.7725887 * jax.random.uniform(seeds[3], (MATS, D, D), jnp.float32) ** shard_levels(seeds[3], (MATS, D, D), ((1, 64), (2, 2)), -0.2, 0.2)), 0.25, 4.0)
    left_stat = draw_left_stat(jax.random.fold_in(seeds[8], 71), 0)
    right_stat = draw_right_stat(jax.random.fold_in(seeds[8], 71), 0)
    left_basis = draw_left_basis(jax.random.fold_in(seeds[8], 71), 0)
    right_basis = draw_right_basis(jax.random.fold_in(seeds[8], 71), 0)
    return {"weights": weights, "gradient": gradient, "first_moment": first_moment, "second_moment": second_moment, "left_stat": left_stat, "right_stat": right_stat, "left_basis": left_basis, "right_basis": right_basis}


BETA_ONE = 0.9
BETA_TWO = 0.99
BETA_STAT = 0.95
ADAM_EPS = 1e-08
STEP_RATE = 0.01
NORM_EPS = 1e-06
COEF_A = 3.4445
COEF_B = -4.775
COEF_C = 2.0315

def product(left, right):
    return jnp.dot(left, right, precision=lax.Precision.HIGHEST, preferred_element_type=jnp.float32)

def orthogonalize(power):
    iterate = power / jnp.sqrt(jnp.sum(power * power) + NORM_EPS)
    for step in range(NS_STEPS):
        square = product(iterate.T, iterate)
        cubic = product(iterate, square)
        fourth = product(iterate.T, cubic)
        quintic = product(iterate, fourth)
        iterate = COEF_A * iterate + COEF_B * cubic + COEF_C * quintic
    return iterate

def soap_single(packed):
    weight, grad, first, second, lstat, rstat, lbasis, rbasis = packed
    width = grad.shape[0]
    rotated = product(product(lbasis.T, grad), rbasis)
    first_new = BETA_ONE * first + (1.0 - BETA_ONE) * rotated
    second_new = BETA_TWO * second + (1.0 - BETA_TWO) * rotated * rotated
    direction = first_new / (jnp.sqrt(second_new) + ADAM_EPS)
    update = product(product(lbasis, direction), rbasis.T)
    weight_new = weight - STEP_RATE * update
    lstat_new = BETA_STAT * lstat + (1.0 - BETA_STAT) / width * product(grad, grad.T)
    rstat_new = BETA_STAT * rstat + (1.0 - BETA_STAT) / width * product(grad.T, grad)
    lbasis_new = orthogonalize(product(lstat_new, lbasis))
    rbasis_new = orthogonalize(product(rstat_new, rbasis))
    return (weight_new, first_new, second_new, lstat_new, rstat_new, lbasis_new, rbasis_new)

def reference(weights, gradient, first_moment, second_moment, left_stat, right_stat, left_basis, right_basis):
    result = lax.map(soap_single, (weights, gradient, first_moment, second_moment, left_stat, right_stat, left_basis, right_basis))
    return (result[0], result[1], result[2], result[3], result[4], result[5], result[6])
```

```python
import functools

import jax
import jax.numpy as jnp
from jax import lax
from jax.experimental import pallas as pl
from jax.experimental.pallas import tpu as pltpu
from jax.sharding import PartitionSpec as P

NS_STEPS = 5

BETA_ONE = 0.9
BETA_TWO = 0.99
BETA_STAT = 0.95
ADAM_EPS = 1e-08
STEP_RATE = 0.01
NORM_EPS = 1e-06
COEF_A = 3.4445
COEF_B = -4.775
COEF_C = 2.0315

MESH = pl.DeviceIdType.MESH
NN = (((1,), (0,)), ((), ()))
NT = (((1,), (1,)), ((), ()))

GRAD, LBAS, RBAS, LSTAT, RSTAT, ROT, DIR, UPD, NLSTAT, NRSTAT, NLBAS, NRBAS = range(12)


def split(value):
    head = value.astype(jnp.bfloat16)
    return head, (value - head.astype(jnp.float32)).astype(jnp.bfloat16)


def product(left, right, form):
    (lh, ll), (rh, rl) = left, right
    dot = functools.partial(
        lax.dot_general, dimension_numbers=form, preferred_element_type=jnp.float32
    )
    return dot(lh, rh) + (dot(lh, rl) + dot(ll, rh))


def kernel(
    n_shard,
    n_tensor,
    grad,
    first,
    second,
    weights,
    lstat,
    rstat,
    lbasis,
    rbasis,
    out_weights,
    out_first,
    out_second,
    out_lstat,
    out_rstat,
    out_lbasis,
    out_rbasis,
    g_own,
    basis_own,
    stat_own,
    dir_own,
    rot_send,
    upd_send,
    rot_recv,
    dir_send,
    upd_recv,
    moments,
    iterate,
    work,
    g_head,
    g_tail,
    b_head,
    b_tail,
    x_head,
    x_tail,
    s_head,
    s_tail,
    send_sem,
    recv_sem,
    load_sem,
):
    order = n_shard * n_tensor
    mats, rows, cols = grad.shape
    width = g_own.shape[1]
    half = width // 2
    shard, tensor = lax.axis_index("shard"), lax.axis_index("tensor")
    me = shard * n_tensor + tensor

    def place(d):
        return d // n_tensor, lax.rem(d, n_tensor)

    def block(d):
        s, t = place(d)
        return (
            pl.ds(pl.multiple_of(s * rows, rows), rows),
            pl.ds(pl.multiple_of(t * cols, cols), cols),
        )

    def to_owners(source, target, index):
        mine = block(me)
        pltpu.make_async_copy(source.at[me], target.at[mine], recv_sem.at[index]).start()

        def send(k, carry):
            d = lax.rem(me + k, order)
            pltpu.make_async_remote_copy(
                src_ref=source.at[d],
                dst_ref=target.at[mine],
                send_sem=send_sem.at[index],
                recv_sem=recv_sem.at[index],
                device_id=place(d),
                device_id_type=MESH,
            ).start()
            return carry

        lax.fori_loop(1, order, send, 0)

    def to_rows(source, target, index):
        pltpu.make_async_copy(source.at[block(me)], target.at[me], recv_sem.at[index]).start()

        def send(k, carry):
            d = lax.rem(me + k, order)
            pltpu.make_async_remote_copy(
                src_ref=source.at[block(d)],
                dst_ref=target.at[me],
                send_sem=send_sem.at[index],
                recv_sem=recv_sem.at[index],
                device_id=place(d),
                device_id_type=MESH,
            ).start()
            return carry

        lax.fori_loop(1, order, send, 0)

    def arrived(target, index):
        pltpu.make_async_remote_copy(
            src_ref=target,
            dst_ref=target,
            send_sem=send_sem.at[index],
            recv_sem=recv_sem.at[index],
            device_id=place(lax.rem(me + 1, order)),
            device_id_type=MESH,
        ).wait_recv()

    def chunks(body):
        def step(i, carry):
            body(pl.ds(pl.multiple_of(i * half, half), half))
            return carry

        lax.fori_loop(0, 2, step, 0)

    barrier = pltpu.get_barrier_semaphore()

    def greet(k, carry):
        pl.semaphore_signal(
            barrier, inc=1, device_id=place(lax.rem(me + k, order)), device_id_type=MESH
        )
        return carry

    lax.fori_loop(1, order, greet, 0)
    pl.semaphore_wait(barrier, order - 1)

    to_owners(grad, g_own, GRAD)
    to_owners(lbasis, basis_own.at[0], LBAS)
    to_owners(rbasis, basis_own.at[1], RBAS)
    to_owners(lstat, stat_own.at[0], LSTAT)
    to_owners(rstat, stat_own.at[1], RSTAT)
    loads = [
        pltpu.make_async_copy(source, moments.at[i], load_sem.at[i])
        for i, source in enumerate((first, second, weights))
    ]
    for load in loads:
        load.start()

    arrived(g_own, GRAD)
    scale = (1.0 - BETA_STAT) / width
    g_head[0], g_tail[0] = split(g_own[...])
    g_head[1], g_tail[1] = split(g_own[...].T)

    def gram(side, carry):
        def rows_of(r):
            full = g_head[side], g_tail[side]
            part = g_head[side, r, :], g_tail[side, r, :]
            work[side, r, :] = scale * product(part, full, NT)

        chunks(rows_of)
        return carry

    lax.fori_loop(0, 2, gram, 0)

    arrived(basis_own.at[0], LBAS)
    b_head[0], b_tail[0] = split(basis_own[0])
    x_head[0], x_tail[0] = split(basis_own[0].T)

    def left_rotate(r):
        part = product((x_head[0, r, :], x_tail[0, r, :]), (g_head[0], g_tail[0]), NN)
        s_head[r, :], s_tail[r, :] = split(part)

    chunks(left_rotate)
    arrived(basis_own.at[1], RBAS)
    b_head[1], b_tail[1] = split(basis_own[1])

    def right_rotate(r):
        rot_send[r, :] = product(
            (s_head[r, :], s_tail[r, :]), (b_head[1], b_tail[1]), NN
        )

    chunks(right_rotate)
    to_rows(rot_send, rot_recv, ROT)

    def power(side, carry):
        arrived(stat_own.at[side], LSTAT + side)
        stat_own[side] = BETA_STAT * stat_own[side] + work[side]
        s_head[...], s_tail[...] = split(stat_own[side])

        def rows_of(r):
            iterate[side, r, :] = product(
                (s_head[r, :], s_tail[r, :]), (b_head[side], b_tail[side]), NN
            )

        chunks(rows_of)
        for which, target in enumerate((out_lstat, out_rstat)):

            @pl.when(side == which)
            def _():
                to_rows(stat_own.at[which], target, NLSTAT + which)

        value = iterate[side]
        value = value / jnp.sqrt(jnp.sum(value * value) + NORM_EPS)
        iterate[side] = value
        x_head[side], x_tail[side] = split(value)
        return carry

    lax.fori_loop(0, 2, power, 0)

    def newton(side):
        def step(_, carry):
            def squares(r):
                full = x_head[side], x_tail[side]
                value = product((x_head[side, r, :], x_tail[side, r, :]), full, NT)
                work[0, r, :] = value
                s_head[r, :], s_tail[r, :] = split(value)

            chunks(squares)

            def polynomial(r):
                fourth = product((s_head[r, :], s_tail[r, :]), (s_head[...], s_tail[...]), NN)
                value = COEF_B * work[0, r, :] + COEF_C * fourth
                g_head[0, r, :], g_tail[0, r, :] = split(value)

            chunks(polynomial)

            def combine(r):
                full = x_head[side], x_tail[side]
                value = product((g_head[0, r, :], g_tail[0, r, :]), full, NN)
                iterate[side, r, :] = COEF_A * iterate[side, r, :] + value

            chunks(combine)
            x_head[side], x_tail[side] = split(iterate[side])
            return carry

        lax.fori_loop(0, NS_STEPS, step, 0)

    def refresh(side, carry):
        newton(side)
        for which, target in enumerate((out_lbasis, out_rbasis)):

            @pl.when(side == which)
            def _():
                to_rows(iterate.at[which], target, NLBAS + which)

        @pl.when(side == 0)
        def _():
            arrived(rot_recv, ROT)
            for load in loads:
                load.wait()

            def adam(i, inner):
                m = pl.ds(i * 8, 8)
                rotated = rot_recv[m]
                new_first = BETA_ONE * moments[0, m] + (1.0 - BETA_ONE) * rotated
                new_second = BETA_TWO * moments[1, m] + (1.0 - BETA_TWO) * rotated * rotated
                out_first[m] = new_first
                out_second[m] = new_second
                dir_send[m] = new_first / (jnp.sqrt(new_second) + ADAM_EPS)
                return inner

            lax.fori_loop(0, mats // 8, adam, 0)
            to_owners(dir_send, dir_own, DIR)

        return carry

    lax.fori_loop(0, 2, refresh, 0)

    arrived(dir_own, DIR)
    g_head[1], g_tail[1] = split(dir_own[...])

    def left_back(r):
        part = product((b_head[0, r, :], b_tail[0, r, :]), (g_head[1], g_tail[1]), NN)
        s_head[r, :], s_tail[r, :] = split(part)

    chunks(left_back)

    def right_back(r):
        upd_send[r, :] = product(
            (s_head[r, :], s_tail[r, :]), (b_head[1], b_tail[1]), NT
        )

    chunks(right_back)
    to_rows(upd_send, upd_recv, UPD)
    arrived(upd_recv, UPD)

    def descend(i, carry):
        m = pl.ds(i * 8, 8)
        out_weights[m] = moments[2, m] - STEP_RATE * upd_recv[m]
        return carry

    lax.fori_loop(0, mats // 8, descend, 0)

    arrived(out_lstat, NLSTAT)
    arrived(out_rstat, NRSTAT)
    arrived(out_lbasis, NLBAS)
    arrived(out_rbasis, NRBAS)

    def sent(index, carry):
        part = rot_recv.at[pl.ds(0, order - 1)]
        pltpu.make_async_remote_copy(
            src_ref=part,
            dst_ref=part,
            send_sem=send_sem.at[index],
            recv_sem=recv_sem.at[index],
            device_id=place(lax.rem(me + 1, order)),
            device_id_type=MESH,
        ).wait_send()
        return carry

    lax.fori_loop(0, 12, sent, 0)


def per_device(
    weights, gradient, first_moment, second_moment, left_stat, right_stat, left_basis, right_basis
):
    n_shard, n_tensor = lax.axis_size("shard"), lax.axis_size("tensor")
    mats, rows, cols = gradient.shape
    width = rows * n_shard
    f32, bf16 = jnp.float32, jnp.bfloat16
    kept = jax.ShapeDtypeStruct((mats, rows, cols), f32)
    vmem = pl.BlockSpec(memory_space=pltpu.VMEM)

    def whole(*lead, dtype=f32):
        return pltpu.VMEM((*lead, width, width), dtype)

    def strip(*lead):
        return pltpu.VMEM((*lead, mats, rows, cols), f32)

    return pl.pallas_call(
        functools.partial(kernel, n_shard, n_tensor),
        out_shape=(kept,) * 7,
        in_specs=[pl.BlockSpec(memory_space=pl.ANY)] * 8,
        out_specs=[vmem] * 7,
        scratch_shapes=[
            whole(),
            whole(2),
            whole(2),
            whole(),
            whole(),
            whole(),
            strip(),
            strip(),
            strip(),
            strip(3),
            whole(2),
            whole(2),
            *[whole(2, dtype=bf16) for _ in range(6)],
            *[whole(dtype=bf16) for _ in range(2)],
            pltpu.SemaphoreType.DMA((12,)),
            pltpu.SemaphoreType.DMA((12,)),
            pltpu.SemaphoreType.DMA((3,)),
        ],
        compiler_params=pltpu.CompilerParams(
            collective_id=0, has_side_effects=True, vmem_limit_bytes=40 * 1024 * 1024
        ),
        name="soap_step",
    )(
        gradient,
        first_moment,
        second_moment,
        weights,
        left_stat,
        right_stat,
        left_basis,
        right_basis,
    )


def solution(mesh):
    spec = P(None, "shard", "tensor")
    return jax.shard_map(
        per_device, mesh=mesh, in_specs=(spec,) * 8, out_specs=(spec,) * 7, check_vma=False
    )
```

```python
import functools

import jax
import jax.numpy as jnp
from jax import lax
from jax.experimental import pallas as pl
from jax.experimental.pallas import tpu as pltpu
from jax.sharding import PartitionSpec as P

NS_STEPS = 5

BETA_ONE = 0.9
BETA_TWO = 0.99
BETA_STAT = 0.95
ADAM_EPS = 1e-08
STEP_RATE = 0.01
NORM_EPS = 1e-06
COEF_A = 3.4445
COEF_B = -4.775
COEF_C = 2.0315

STRIDE = 37
LANES = 128
MESH = pl.DeviceIdType.MESH
NN = (((1,), (0,)), ((), ()))
NT = (((1,), (1,)), ((), ()))

GRAD, LBAS, RBAS, LSTAT, RSTAT, ROT, DIR, UPD, NLSTAT, NRSTAT, NLBAS, NRBAS = range(12)


def split(value):
    head = value.astype(jnp.bfloat16)
    return head, (value - head.astype(jnp.float32)).astype(jnp.bfloat16)


def product(left, right, form):
    (lh, ll), (rh, rl) = left, right
    dot = functools.partial(
        lax.dot_general, dimension_numbers=form, preferred_element_type=jnp.float32
    )
    return dot(lh, rh) + (dot(lh, rl) + dot(ll, rh))


def kernel(
    n_shard,
    n_tensor,
    grad,
    first,
    second,
    weights,
    lstat,
    rstat,
    lbasis,
    rbasis,
    out_weights,
    out_first,
    out_second,
    out_lstat,
    out_rstat,
    out_lbasis,
    out_rbasis,
    g_own,
    basis_own,
    stat_own,
    dir_own,
    rot_send,
    upd_send,
    rot_recv,
    dir_send,
    upd_recv,
    moments,
    iterate,
    work,
    g_head,
    g_tail,
    b_head,
    b_tail,
    x_head,
    x_tail,
    s_head,
    s_tail,
    send_sem,
    recv_sem,
    load_sem,
):
    order = n_shard * n_tensor
    mats, rows, cols = grad.shape
    width = g_own.shape[1]
    half = width // 2
    shard, tensor = lax.axis_index("shard"), lax.axis_index("tensor")
    me = shard * n_tensor + tensor

    def to_peers(send):
        def around(j, carry):
            s = lax.rem(shard + j * STRIDE, n_shard)
            for t in range(n_tensor):
                send(s * n_tensor + t, s, t)
            return carry

        for t in range(1, n_tensor):
            other = lax.rem(tensor + t, n_tensor)
            send(shard * n_tensor + other, shard, other)
        lax.fori_loop(1, n_shard, around, 0)

    def block(s, t):
        return (
            pl.ds(pl.multiple_of(s * rows, rows), rows),
            pl.ds(pl.multiple_of(t * cols, cols), cols),
        )

    def exchange(source_of, target, own, index):
        pltpu.make_async_copy(own, target, recv_sem.at[index]).start()

        def send(d, s, t):
            pltpu.make_async_remote_copy(
                src_ref=source_of(d, s, t),
                dst_ref=target,
                send_sem=send_sem.at[index],
                recv_sem=recv_sem.at[index],
                device_id=(s, t),
                device_id_type=MESH,
            ).start()

        to_peers(send)

    def to_owners(source, target, index):
        exchange(
            lambda d, s, t: source.at[d], target.at[block(shard, tensor)], source.at[me], index
        )

    def to_rows(source, target, index):
        exchange(
            lambda d, s, t: source.at[block(s, t)],
            target.at[me],
            source.at[block(shard, tensor)],
            index,
        )

    blocks = width // LANES
    row_block = shard * rows // LANES
    wide = cols // LANES
    count = blocks * (blocks + 1) // 2

    def travels(row, lag, side):
        if blocks % 2:
            return lag <= blocks // 2
        late = row >= blocks // 2 if side else row < blocks // 2
        return (lag < blocks // 2) | ((lag == blocks // 2) & late)

    def stat_parts(side, body):
        flags = []
        for i in range(wide):
            lag = lax.rem(tensor * wide + i - row_block + blocks, blocks)
            flags.append(travels(row_block, lag, side))
        for i, flag in enumerate(flags):
            pl.when(flag)(functools.partial(body, i * LANES, LANES))

    def stat_to_owners(source, side):
        target = stat_own.at[side]
        down, across = block(shard, tensor)

        def body(start, lanes):
            part = pl.ds(start, lanes)
            to = target.at[down, pl.ds(pl.multiple_of(tensor * cols + start, lanes), lanes)]
            exchange(
                lambda d, s, t: source.at[d, :, part],
                to,
                source.at[me, :, part],
                LSTAT + side,
            )

        stat_parts(side, body)

    def mirror(side):
        for row in range(blocks):
            for lag in range(blocks):
                if not travels(row, lag, side):
                    column = (row + lag) % blocks
                    down = slice(row * LANES, (row + 1) * LANES)
                    across = slice(column * LANES, (column + 1) * LANES)
                    stat_own[side, down, across] = stat_own[side, across, down].T

    def arrived(target, index):
        pltpu.make_async_remote_copy(
            src_ref=target,
            dst_ref=target,
            send_sem=send_sem.at[index],
            recv_sem=recv_sem.at[index],
            device_id=(lax.rem(shard + 1, n_shard), tensor),
            device_id_type=MESH,
        ).wait_recv()

    def chunks(body):
        def step(i, carry):
            body(pl.ds(pl.multiple_of(i * half, half), half))
            return carry

        lax.fori_loop(0, 2, step, 0)

    barrier = pltpu.get_barrier_semaphore()

    to_peers(
        lambda d, s, t: pl.semaphore_signal(
            barrier, inc=1, device_id=(s, t), device_id_type=MESH
        )
    )
    pl.semaphore_wait(barrier, order - 1)

    to_owners(grad, g_own, GRAD)
    to_owners(lbasis, basis_own.at[0], LBAS)
    to_owners(rbasis, basis_own.at[1], RBAS)
    stat_to_owners(lstat, 0)
    stat_to_owners(rstat, 1)
    loads = [
        pltpu.make_async_copy(source, moments.at[i], load_sem.at[i])
        for i, source in enumerate((first, second, weights))
    ]
    for load in loads:
        load.start()

    arrived(g_own, GRAD)
    scale = (1.0 - BETA_STAT) / width
    g_head[0], g_tail[0] = split(g_own[...])
    g_head[1], g_tail[1] = split(g_own[...].T)

    def gram(side, carry):
        def rows_of(r):
            full = g_head[side], g_tail[side]
            part = g_head[side, r, :], g_tail[side, r, :]
            work[side, r, :] = scale * product(part, full, NT)

        chunks(rows_of)
        return carry

    lax.fori_loop(0, 2, gram, 0)

    arrived(basis_own.at[0], LBAS)
    b_head[0], b_tail[0] = split(basis_own[0])
    x_head[0], x_tail[0] = split(basis_own[0].T)

    def left_rotate(r):
        part = product((x_head[0, r, :], x_tail[0, r, :]), (g_head[0], g_tail[0]), NN)
        s_head[r, :], s_tail[r, :] = split(part)

    chunks(left_rotate)
    arrived(basis_own.at[1], RBAS)
    b_head[1], b_tail[1] = split(basis_own[1])

    def right_rotate(r):
        rot_send[r, :] = product(
            (s_head[r, :], s_tail[r, :]), (b_head[1], b_tail[1]), NN
        )

    chunks(right_rotate)
    to_rows(rot_send, rot_recv, ROT)

    def power(side, carry):
        arrived(stat_own.at[side, pl.ds(0, count * LANES * LANES // width)], LSTAT + side)
        for which in range(2):
            pl.when(side == which)(functools.partial(mirror, which))
        stat_own[side] = BETA_STAT * stat_own[side] + work[side]
        s_head[...], s_tail[...] = split(stat_own[side])

        def rows_of(r):
            iterate[side, r, :] = product(
                (s_head[r, :], s_tail[r, :]), (b_head[side], b_tail[side]), NN
            )

        chunks(rows_of)
        for which, target in enumerate((out_lstat, out_rstat)):

            @pl.when(side == which)
            def _():
                to_rows(stat_own.at[which], target, NLSTAT + which)

        value = iterate[side]
        value = value / jnp.sqrt(jnp.sum(value * value) + NORM_EPS)
        iterate[side] = value
        x_head[side], x_tail[side] = split(value)
        return carry

    lax.fori_loop(0, 2, power, 0)

    def newton(side):
        def step(_, carry):
            def squares(r):
                full = x_head[side], x_tail[side]
                value = product((x_head[side, r, :], x_tail[side, r, :]), full, NT)
                work[0, r, :] = value
                s_head[r, :], s_tail[r, :] = split(value)

            chunks(squares)

            def polynomial(r):
                fourth = product((s_head[r, :], s_tail[r, :]), (s_head[...], s_tail[...]), NN)
                value = COEF_B * work[0, r, :] + COEF_C * fourth
                g_head[0, r, :], g_tail[0, r, :] = split(value)

            chunks(polynomial)

            def combine(r):
                full = x_head[side], x_tail[side]
                value = product((g_head[0, r, :], g_tail[0, r, :]), full, NN)
                iterate[side, r, :] = COEF_A * iterate[side, r, :] + value

            chunks(combine)
            x_head[side], x_tail[side] = split(iterate[side])
            return carry

        lax.fori_loop(0, NS_STEPS, step, 0)

    def refresh(side, carry):
        newton(side)
        for which, target in enumerate((out_lbasis, out_rbasis)):

            @pl.when(side == which)
            def _():
                to_rows(iterate.at[which], target, NLBAS + which)

        @pl.when(side == 0)
        def _():
            arrived(rot_recv, ROT)
            for load in loads:
                load.wait()

            def adam(i, inner):
                m = pl.ds(i * 8, 8)
                rotated = rot_recv[m]
                new_first = BETA_ONE * moments[0, m] + (1.0 - BETA_ONE) * rotated
                new_second = BETA_TWO * moments[1, m] + (1.0 - BETA_TWO) * rotated * rotated
                out_first[m] = new_first
                out_second[m] = new_second
                dir_send[m] = new_first / (jnp.sqrt(new_second) + ADAM_EPS)
                return inner

            lax.fori_loop(0, mats // 8, adam, 0)
            to_owners(dir_send, dir_own, DIR)

        return carry

    lax.fori_loop(0, 2, refresh, 0)

    arrived(dir_own, DIR)
    g_head[1], g_tail[1] = split(dir_own[...])

    def left_back(r):
        part = product((b_head[0, r, :], b_tail[0, r, :]), (g_head[1], g_tail[1]), NN)
        s_head[r, :], s_tail[r, :] = split(part)

    chunks(left_back)

    def right_back(r):
        upd_send[r, :] = product(
            (s_head[r, :], s_tail[r, :]), (b_head[1], b_tail[1]), NT
        )

    chunks(right_back)
    to_rows(upd_send, upd_recv, UPD)
    arrived(upd_recv, UPD)

    def descend(i, carry):
        m = pl.ds(i * 8, 8)
        out_weights[m] = moments[2, m] - STEP_RATE * upd_recv[m]
        return carry

    lax.fori_loop(0, mats // 8, descend, 0)

    arrived(out_lstat, NLSTAT)
    arrived(out_rstat, NRSTAT)
    arrived(out_lbasis, NLBAS)
    arrived(out_rbasis, NRBAS)

    def sent(part, index):
        pltpu.make_async_remote_copy(
            src_ref=part,
            dst_ref=part,
            send_sem=send_sem.at[index],
            recv_sem=recv_sem.at[index],
            device_id=(lax.rem(shard + 1, n_shard), tensor),
            device_id_type=MESH,
        ).wait_send()

    for index in range(12):
        if index not in (LSTAT, RSTAT):
            sent(rot_recv.at[pl.ds(0, order - 1)], index)
    for side in range(2):
        stat_parts(
            side,
            lambda start, lanes: sent(
                rot_recv.at[pl.ds(0, order - 1), :, pl.ds(0, lanes)], LSTAT + side
            ),
        )


def keep(*refs):
    count = len(refs) // 2
    sem = refs[-1]
    copies = [
        pltpu.make_async_copy(source, target, sem.at[i])
        for i, (source, target) in enumerate(zip(refs[:count], refs[count:]))
    ]
    for copy in copies:
        copy.start()
    for copy in copies:
        copy.wait()


def per_device(
    weights, gradient, first_moment, second_moment, left_stat, right_stat, left_basis, right_basis
):
    n_shard, n_tensor = lax.axis_size("shard"), lax.axis_size("tensor")
    mats, rows, cols = gradient.shape
    width = rows * n_shard
    f32, bf16 = jnp.float32, jnp.bfloat16
    kept = jax.ShapeDtypeStruct((mats, rows, cols), f32)
    vmem = pl.BlockSpec(memory_space=pltpu.VMEM)
    hbm = pl.BlockSpec(memory_space=pltpu.HBM)

    def whole(*lead, dtype=f32):
        return pltpu.VMEM((*lead, width, width), dtype)

    def strip(*lead):
        return pltpu.VMEM((*lead, mats, rows, cols), f32)

    results = pl.pallas_call(
        functools.partial(kernel, n_shard, n_tensor),
        out_shape=(kept,) * 7,
        in_specs=[hbm] * 8,
        out_specs=[vmem] * 7,
        scratch_shapes=[
            whole(),
            whole(2),
            whole(2),
            whole(),
            whole(),
            whole(),
            strip(),
            strip(),
            strip(),
            strip(3),
            whole(2),
            whole(2),
            *[whole(2, dtype=bf16) for _ in range(6)],
            *[whole(dtype=bf16) for _ in range(2)],
            pltpu.SemaphoreType.DMA((12,)),
            pltpu.SemaphoreType.DMA((12,)),
            pltpu.SemaphoreType.DMA((3,)),
        ],
        compiler_params=pltpu.CompilerParams(
            collective_id=0, has_side_effects=True, vmem_limit_bytes=46 * 1024 * 1024
        ),
        name="soap_step",
    )(
        gradient,
        first_moment,
        second_moment,
        weights,
        left_stat,
        right_stat,
        left_basis,
        right_basis,
    )
    return pl.pallas_call(
        keep,
        out_shape=(kept,) * 7,
        in_specs=[vmem] * 7,
        out_specs=[hbm] * 7,
        scratch_shapes=[pltpu.SemaphoreType.DMA((7,))],
        compiler_params=pltpu.CompilerParams(vmem_limit_bytes=1024 * 1024),
        name="keep",
    )(*results)


def solution(mesh):
    spec = P(None, "shard", "tensor")
    return jax.shard_map(
        per_device, mesh=mesh, in_specs=(spec,) * 8, out_specs=(spec,) * 7, check_vma=False
    )
```

```python
import functools
import itertools

import jax
import jax.numpy as jnp
from jax import lax
from jax.experimental import pallas as pl
from jax.experimental.pallas import tpu as pltpu
from jax.sharding import PartitionSpec as P

NS_STEPS = 5

BETA_ONE = 0.9
BETA_TWO = 0.99
BETA_STAT = 0.95
ADAM_EPS = 1e-08
STEP_RATE = 0.01
NORM_EPS = 1e-06
COEF_A = 3.4445
COEF_B = -4.775
COEF_C = 2.0315

STRIDE = 37
LANES = 128
PARTS = 4
MESH = pl.DeviceIdType.MESH
NN = (((1,), (0,)), ((), ()))
NT = (((1,), (1,)), ((), ()))

GRAD, LBAS, RBAS, LSTAT, RSTAT, ROT, DIR, UPD, NLSTAT, NRSTAT, NLBAS, NRBAS = range(12)


def split(value):
    head = value.astype(jnp.bfloat16)
    return head, (value - head.astype(jnp.float32)).astype(jnp.bfloat16)


def product(left, right, form):
    (lh, ll), (rh, rl) = left, right
    dot = functools.partial(
        lax.dot_general, dimension_numbers=form, preferred_element_type=jnp.float32
    )
    return dot(lh, rh) + (dot(lh, rl) + dot(ll, rh))


def kernel(
    n_shard,
    n_tensor,
    grad,
    first,
    second,
    weights,
    lstat,
    rstat,
    lbasis,
    rbasis,
    out_weights,
    out_first,
    out_second,
    out_lstat,
    out_rstat,
    out_lbasis,
    out_rbasis,
    g_own,
    basis_own,
    stat_own,
    dir_own,
    rot_send,
    upd_send,
    rot_recv,
    dir_send,
    upd_recv,
    moments,
    iterate,
    work,
    g_head,
    g_tail,
    b_head,
    b_tail,
    x_head,
    x_tail,
    s_head,
    s_tail,
    send_sem,
    recv_sem,
    load_sem,
):
    order = n_shard * n_tensor
    mats, rows, cols = grad.shape
    width = g_own.shape[1]
    half = width // 2
    shard, tensor = lax.axis_index("shard"), lax.axis_index("tensor")
    me = shard * n_tensor + tensor

    stride = STRIDE + tensor * (n_shard - 2 * STRIDE)

    def to_peers(send):
        def around(j, carry):
            s = lax.rem(shard + j * stride, n_shard)
            for t in range(n_tensor):
                send(s * n_tensor + t, s, t)
            return carry

        for t in range(1, n_tensor):
            other = lax.rem(tensor + t, n_tensor)
            send(shard * n_tensor + other, shard, other)
        lax.fori_loop(1, n_shard, around, 0)

    def block(s, t):
        return (
            pl.ds(pl.multiple_of(s * rows, rows), rows),
            pl.ds(pl.multiple_of(t * cols, cols), cols),
        )

    def exchange(source_of, target, own, index):
        pltpu.make_async_copy(own, target, recv_sem.at[index]).start()

        def send(d, s, t):
            pltpu.make_async_remote_copy(
                src_ref=source_of(d, s, t),
                dst_ref=target,
                send_sem=send_sem.at[index],
                recv_sem=recv_sem.at[index],
                device_id=(s, t),
                device_id_type=MESH,
            ).start()

        to_peers(send)

    def to_owners(source, target, index):
        exchange(
            lambda d, s, t: source.at[d], target.at[block(shard, tensor)], source.at[me], index
        )

    def to_rows(source, target, index):
        exchange(
            lambda d, s, t: source.at[block(s, t)],
            target.at[me],
            source.at[block(shard, tensor)],
            index,
        )

    blocks = width // LANES
    row_block = shard * rows // LANES
    wide = cols // LANES
    count = blocks * (blocks + 1) // 2

    def travels(row, lag, side):
        if blocks % 2:
            return lag <= blocks // 2
        late = row >= blocks // 2 if side else row < blocks // 2
        return (lag < blocks // 2) | ((lag == blocks // 2) & late)

    def stat_parts(side, body):
        flags = []
        for i in range(wide):
            lag = lax.rem(tensor * wide + i - row_block + blocks, blocks)
            flags.append(travels(row_block, lag, side))
        for i, flag in enumerate(flags):
            pl.when(flag)(functools.partial(body, i * LANES, LANES))

    def stat_to_owners(source, side):
        target = stat_own.at[side]
        down, across = block(shard, tensor)

        def body(start, lanes):
            part = pl.ds(start, lanes)
            to = target.at[down, pl.ds(pl.multiple_of(tensor * cols + start, lanes), lanes)]
            exchange(
                lambda d, s, t: source.at[d, :, part],
                to,
                source.at[me, :, part],
                LSTAT + side,
            )

        stat_parts(side, body)

    def mirror(side):
        for row in range(blocks):
            for lag in range(blocks):
                if not travels(row, lag, side):
                    column = (row + lag) % blocks
                    down = slice(row * LANES, (row + 1) * LANES)
                    across = slice(column * LANES, (column + 1) * LANES)
                    stat_own[side, down, across] = stat_own[side, across, down].T

    def arrived(target, index):
        pltpu.make_async_remote_copy(
            src_ref=target,
            dst_ref=target,
            send_sem=send_sem.at[index],
            recv_sem=recv_sem.at[index],
            device_id=(lax.rem(shard + 1, n_shard), tensor),
            device_id_type=MESH,
        ).wait_recv()

    def chunks(body):
        def step(i, carry):
            body(pl.ds(pl.multiple_of(i * half, half), half))
            return carry

        lax.fori_loop(0, 2, step, 0)

    barrier = pltpu.get_barrier_semaphore()

    edge = round(n_shard ** (1 / 3))
    here = shard // (edge * edge), lax.rem(shard // edge, edge), lax.rem(shard, edge)
    along = [[lax.rem(at + step, edge) for step in range(edge)] for at in here]
    steps = sorted(
        itertools.product(range(edge), repeat=3),
        key=lambda step: -sum(min(i, edge - i) for i in step),
    )
    for i, j, k in steps:
        s = (along[0][i] * edge + along[1][j]) * edge + along[2][k]
        for t in range(n_tensor):
            if (i, j, k) == (0, 0, 0):
                if t == 0:
                    continue
                t = lax.rem(tensor + t, n_tensor)
            pl.semaphore_signal(barrier, inc=1, device_id=(s, t), device_id_type=MESH)
    pl.semaphore_wait(barrier, order - 1)

    to_owners(grad, g_own, GRAD)
    to_owners(lbasis, basis_own.at[0], LBAS)
    to_owners(rbasis, basis_own.at[1], RBAS)
    stat_to_owners(lstat, 0)
    stat_to_owners(rstat, 1)
    loads = [
        pltpu.make_async_copy(source, moments.at[i], load_sem.at[i])
        for i, source in enumerate((first, second, weights))
    ]
    for load in loads:
        load.start()

    arrived(g_own, GRAD)
    scale = (1.0 - BETA_STAT) / width
    g_head[0], g_tail[0] = split(g_own[...])
    g_head[1], g_tail[1] = split(g_own[...].T)

    def gram(side, carry):
        def rows_of(r):
            full = g_head[side], g_tail[side]
            part = g_head[side, r, :], g_tail[side, r, :]
            work[side, r, :] = scale * product(part, full, NT)

        chunks(rows_of)
        return carry

    lax.fori_loop(0, 2, gram, 0)

    arrived(basis_own.at[0], LBAS)
    b_head[0], b_tail[0] = split(basis_own[0])
    x_head[0], x_tail[0] = split(basis_own[0].T)

    def left_rotate(r):
        part = product((x_head[0, r, :], x_tail[0, r, :]), (g_head[0], g_tail[0]), NN)
        s_head[r, :], s_tail[r, :] = split(part)

    chunks(left_rotate)
    arrived(basis_own.at[1], RBAS)
    b_head[1], b_tail[1] = split(basis_own[1])

    def right_rotate(r):
        rot_send[r, :] = product(
            (s_head[r, :], s_tail[r, :]), (b_head[1], b_tail[1]), NN
        )

    chunks(right_rotate)
    to_rows(rot_send, rot_recv, ROT)

    def power(side, carry):
        arrived(stat_own.at[side, pl.ds(0, count * LANES * LANES // width)], LSTAT + side)
        for which in range(2):
            pl.when(side == which)(functools.partial(mirror, which))
        stat_own[side] = BETA_STAT * stat_own[side] + work[side]
        s_head[...], s_tail[...] = split(stat_own[side])

        def rows_of(r):
            iterate[side, r, :] = product(
                (s_head[r, :], s_tail[r, :]), (b_head[side], b_tail[side]), NN
            )

        chunks(rows_of)
        for which, target in enumerate((out_lstat, out_rstat)):

            @pl.when(side == which)
            def _():
                to_rows(stat_own.at[which], target, NLSTAT + which)

        value = iterate[side]
        value = value / jnp.sqrt(jnp.sum(value * value) + NORM_EPS)
        iterate[side] = value
        x_head[side], x_tail[side] = split(value)
        return carry

    lax.fori_loop(0, 2, power, 0)

    def newton(side):
        def step(_, carry):
            def squares(r):
                full = x_head[side], x_tail[side]
                value = product((x_head[side, r, :], x_tail[side, r, :]), full, NT)
                work[0, r, :] = value
                s_head[r, :], s_tail[r, :] = split(value)

            chunks(squares)

            def polynomial(r):
                fourth = product((s_head[r, :], s_tail[r, :]), (s_head[...], s_tail[...]), NN)
                value = COEF_B * work[0, r, :] + COEF_C * fourth
                g_head[0, r, :], g_tail[0, r, :] = split(value)

            chunks(polynomial)

            def combine(r):
                full = x_head[side], x_tail[side]
                value = product((g_head[0, r, :], g_tail[0, r, :]), full, NN)
                iterate[side, r, :] = COEF_A * iterate[side, r, :] + value

            chunks(combine)
            x_head[side], x_tail[side] = split(iterate[side])
            return carry

        lax.fori_loop(0, NS_STEPS, step, 0)

    def refresh(side, carry):
        newton(side)
        for which, target in enumerate((out_lbasis, out_rbasis)):

            @pl.when(side == which)
            def _():
                to_rows(iterate.at[which], target, NLBAS + which)

        @pl.when(side == 0)
        def _():
            arrived(rot_recv, ROT)
            for load in loads:
                load.wait()

            def adam(i, inner):
                m = pl.ds(i * 8, 8)
                rotated = rot_recv[m]
                new_first = BETA_ONE * moments[0, m] + (1.0 - BETA_ONE) * rotated
                new_second = BETA_TWO * moments[1, m] + (1.0 - BETA_TWO) * rotated * rotated
                out_first[m] = new_first
                out_second[m] = new_second
                dir_send[m] = new_first / (jnp.sqrt(new_second) + ADAM_EPS)
                return inner

            lax.fori_loop(0, mats // 8, adam, 0)
            to_owners(dir_send, dir_own, DIR)

        return carry

    lax.fori_loop(0, 2, refresh, 0)

    arrived(dir_own, DIR)
    g_head[1], g_tail[1] = split(dir_own[...])

    def left_back(r):
        part = product((b_head[0, r, :], b_tail[0, r, :]), (g_head[1], g_tail[1]), NN)
        s_head[r, :], s_tail[r, :] = split(part)

    chunks(left_back)

    def right_back(r):
        upd_send[r, :] = product(
            (s_head[r, :], s_tail[r, :]), (b_head[1], b_tail[1]), NT
        )

    chunks(right_back)
    to_rows(upd_send, upd_recv, UPD)
    arrived(upd_recv, UPD)

    def descend(i, carry):
        m = pl.ds(i * 8, 8)
        out_weights[m] = moments[2, m] - STEP_RATE * upd_recv[m]
        return carry

    lax.fori_loop(0, mats // 8, descend, 0)

    arrived(out_lstat, NLSTAT)
    arrived(out_rstat, NRSTAT)
    arrived(out_lbasis, NLBAS)
    arrived(out_rbasis, NRBAS)

    def sent(part, index):
        pltpu.make_async_remote_copy(
            src_ref=part,
            dst_ref=part,
            send_sem=send_sem.at[index],
            recv_sem=recv_sem.at[index],
            device_id=(lax.rem(shard + 1, n_shard), tensor),
            device_id_type=MESH,
        ).wait_send()

    for index in range(12):
        if index not in (LSTAT, RSTAT):
            sent(rot_recv.at[pl.ds(0, order - 1)], index)
    for side in range(2):
        stat_parts(
            side,
            lambda start, lanes: sent(
                rot_recv.at[pl.ds(0, order - 1), :, pl.ds(0, lanes)], LSTAT + side
            ),
        )


def keep(*refs):
    count = len(refs) // 2
    sem = refs[-1]
    part = refs[0].shape[0] // PARTS
    copies = [
        pltpu.make_async_copy(
            source.at[pl.ds(p * part, part)], target.at[pl.ds(p * part, part)], sem.at[i, p]
        )
        for p in range(PARTS)
        for i, (source, target) in enumerate(zip(refs[:count], refs[count:]))
    ]
    for copy in copies:
        copy.start()
    for copy in copies:
        copy.wait()


def per_device(
    weights, gradient, first_moment, second_moment, left_stat, right_stat, left_basis, right_basis
):
    n_shard, n_tensor = lax.axis_size("shard"), lax.axis_size("tensor")
    mats, rows, cols = gradient.shape
    width = rows * n_shard
    f32, bf16 = jnp.float32, jnp.bfloat16
    kept = jax.ShapeDtypeStruct((mats, rows, cols), f32)
    vmem = pl.BlockSpec(memory_space=pltpu.VMEM)
    hbm = pl.BlockSpec(memory_space=pltpu.HBM)

    def whole(*lead, dtype=f32):
        return pltpu.VMEM((*lead, width, width), dtype)

    def strip(*lead):
        return pltpu.VMEM((*lead, mats, rows, cols), f32)

    results = pl.pallas_call(
        functools.partial(kernel, n_shard, n_tensor),
        out_shape=(kept,) * 7,
        in_specs=[hbm] * 8,
        out_specs=[vmem] * 7,
        scratch_shapes=[
            whole(),
            whole(2),
            whole(2),
            whole(),
            whole(),
            whole(),
            strip(),
            strip(),
            strip(),
            strip(3),
            whole(2),
            whole(2),
            *[whole(2, dtype=bf16) for _ in range(6)],
            *[whole(dtype=bf16) for _ in range(2)],
            pltpu.SemaphoreType.DMA((12,)),
            pltpu.SemaphoreType.DMA((12,)),
            pltpu.SemaphoreType.DMA((3,)),
        ],
        compiler_params=pltpu.CompilerParams(
            collective_id=0, has_side_effects=True, vmem_limit_bytes=46 * 1024 * 1024
        ),
        name="soap_step",
    )(
        gradient,
        first_moment,
        second_moment,
        weights,
        left_stat,
        right_stat,
        left_basis,
        right_basis,
    )
    return pl.pallas_call(
        keep,
        out_shape=(kept,) * 7,
        in_specs=[vmem] * 7,
        out_specs=[hbm] * 7,
        scratch_shapes=[pltpu.SemaphoreType.DMA((7, PARTS))],
        compiler_params=pltpu.CompilerParams(vmem_limit_bytes=1024 * 1024),
        name="keep",
    )(*results)


def solution(mesh):
    spec = P(None, "shard", "tensor")
    return jax.shard_map(
        per_device, mesh=mesh, in_specs=(spec,) * 8, out_specs=(spec,) * 7, check_vma=False
    )
```
